256 devices in a mesh: member: 4 (over x_lo, core), space: 64 (over y, z, x_hi).
Axes of the slice: x: 4 (x_hi: 2, x_lo: 2; x = x_hi * 2 + x_lo), y: 4, z: 8, core: 2. Of those that a mesh axis runs over, the one named last changes fastest.
Arguments:
- mesh_latent: bfloat16 [8, 8192, 1024], P('member', 'space'), may hold values from -6 to 6
- w_hidden: bfloat16 [1024, 1024], replicated, may hold values from -0.1875 to 0.1875
- w_out: bfloat16 [100, 1024], replicated, may hold values from -0.1875 to 0.1875
- target: bfloat16 [100, 32768], P(None, 'space'), may hold values from -6 to 6
- slots: int32 [3, 32768], P(None, 'space'), may hold values from 0 to 383, as said below
- lengths: int32 [64], P('space'), may hold values from 1 to 512, 24576 in all
Outputs:
- grad_hidden: float32 [1024, 1024], P('space')
- grad_mesh: bfloat16 [8, 8192, 1024], P('member', 'space')
The draws below stay inside these ranges and needn't reach their ends.
Inputs may be any that keep to these rules, and one draw needn't show every extreme that they name: The three entries of a column are distinct slots of the padded block of 384 nodes of its tile. `lengths`: local grid positions at or beyond a tile's length are padding.
All inputs are finite; a program needn't handle non-finite values. No bound on the sum of `lengths` on one device may be relied on, other than what follows from the above.
Results may differ from the reference program's by a relative error of at most 0.015.
Values may be sent and summed in bfloat16 or wider, within the bound.
No kernel may reach another device: no remote copies, remote signals or barrier semaphores. Data moves between devices by JAX's collectives and lax.ppermute only.
A program may use at most 64 MiB of HBM per device.

```python
import math
import jax
import jax.numpy as jnp
import numpy as np
from jax import lax

L = 1024
C = 100
MESH_DEV = 128
GRID_DEV = 512
MEMBERS = 8
MESH = 8192
GRID = 32768
N_SPACE = 64


def draw_slots(key, part):
    key_first, key_second, key_third = jax.random.split(key, 3)
    span = 3 * MESH_DEV
    first = jax.random.randint(key_first, (GRID,), 0, span)
    second = (first + 1 + jax.random.randint(key_second, (GRID,), 0, MESH_DEV)) % span
    third = (second + 1 + jax.random.randint(key_third, (GRID,), 0, MESH_DEV)) % span
    return jnp.stack([first, second, third]).astype(jnp.int32)


def steps_of(key, extent, cuts, low, high):
    loudness, own = 1.0, jax.random.fold_in(key, 6)
    for axis_at, parts in cuts:
        steps = jnp.exp(jax.random.uniform(jax.random.fold_in(own, axis_at), (parts,), jnp.float32, low / len(cuts), high / len(cuts)))
        loudness = loudness * jnp.repeat(steps, extent[axis_at] // parts).reshape([-1 if axis == axis_at else 1 for axis in range(len(extent))])
    return loudness


def split_up(count, total, limit, lean):
    loads = [(1 << 20) // math.isqrt(grade ** lean) + 1 for grade in range(2, count + 1)]
    rest, given = total - limit - (count - 1), [1] * (count - 1)
    while rest > 0:
        free = [i for i in range(count - 1) if given[i] < limit]
        pool, left = sum([loads[i] for i in free]), rest
        for i in free:
            addition = min(limit - given[i], max(1, left * loads[i] // pool), rest)
            given[i] = given[i] + addition
            rest = rest - addition
    return np.array([limit] + given)


def uneven_parts(stream_key, number_of, total, most, slope):
    if number_of == 2:
        one = jax.random.randint(stream_key, (), max(1, total - most), min(most, total - 1) + 1)
        return jnp.stack([one, total - one])
    tallies = jnp.asarray(split_up(number_of, total, most, slope), jnp.int32)
    twos = (number_of - 1) // 2
    donor, receiver = tallies[1:1 + 2 * twos:2], tallies[2:2 + 2 * twos:2]
    margin = jnp.minimum(donor - 1, most - receiver)
    passed = jax.random.randint(jax.random.fold_in(stream_key, 1), (twos,), 0, 1 << 20) % (margin + 1)
    tallies = tallies.at[1:1 + 2 * twos:2].set(donor - passed).at[2:2 + 2 * twos:2].set(receiver + passed)
    return tallies[jax.random.permutation(jax.random.fold_in(stream_key, 2), number_of)]


def centred(rng, dims, width, limit, cuts=(), kind=jnp.bfloat16):
    entries = width * jax.random.normal(rng, dims, jnp.float32)
    if cuts:
        entries = entries * steps_of(rng, dims, cuts, -0.22, 0.18)
    return jnp.clip(entries, -limit, limit).astype(kind)


def setup_inputs(seed: int = 0) -> dict:
    keys = jax.random.split(jax.random.key(seed), 7)
    mesh_latent = centred(keys[0], (MEMBERS, MESH, L), 1.0, 6.0, ((0, 4), (1, 64)))
    w_hidden = centred(keys[1], (L, L), L ** -0.5, 0.1875)
    w_out = centred(keys[2], (C, L), L ** -0.5, 0.1875)
    target = centred(keys[3], (C, GRID), 1.0, 6.0, ((1, 64),))
    slots = draw_slots(jax.random.fold_in(keys[6], 71), 0)
    lengths = uneven_parts(keys[5], N_SPACE, N_SPACE * GRID_DEV * 3 // 4, GRID_DEV, 2).astype(jnp.int32)
    return {"mesh_latent": mesh_latent, "w_hidden": w_hidden, "w_out": w_out, "target": target, "slots": slots, "lengths": lengths}


fair_eps = 0.05
smooth_sq = 0.01

def smooth_sign(value):
    return value / jnp.sqrt(value * value + smooth_sq)

def reference(mesh_latent, w_hidden, w_out, target, slots, lengths):
    blocks = mesh_latent.reshape(MEMBERS, N_SPACE, MESH_DEV, L)
    positions = jnp.arange(3 * MESH_DEV, dtype=jnp.int32)
    w_hid = w_hidden.astype(jnp.float32)
    w_prj = w_out.astype(jnp.float32)
    total = MEMBERS

    def step(carry, tile):
        sum_hidden, sum_mesh = carry
        below = (tile + N_SPACE - 1) % N_SPACE
        above = (tile + 1) % N_SPACE
        extended = jnp.concatenate([blocks[:, below], blocks[:, tile], blocks[:, above]], axis=1).astype(jnp.float32)
        start = (tile * GRID_DEV).astype(jnp.int32)
        tile_slots = lax.dynamic_slice_in_dim(slots, start, GRID_DEV, 1)
        counts = jnp.zeros((GRID_DEV, 3 * MESH_DEV), jnp.float32)
        for k in range(3):
            counts = counts + (tile_slots[k][:, None] == positions[None, :]).astype(jnp.float32)
        area = jnp.einsum('gs,msl->mgl', counts, extended).astype(jnp.bfloat16).astype(jnp.float32)
        pre = jnp.einsum('mgl,lj->mgj', area, w_hid)
        hidden = jax.nn.silu(pre).astype(jnp.bfloat16).astype(jnp.float32)
        pred = jnp.einsum('cj,mgj->mcg', w_prj, hidden).astype(jnp.bfloat16).astype(jnp.float32)
        truth = lax.dynamic_slice_in_dim(target, start, GRID_DEV, 1).astype(jnp.float32)
        live = (jnp.arange(GRID_DEV, dtype=jnp.int32) < lengths[tile]).astype(jnp.float32)
        first = smooth_sign(pred - truth[None]) / total
        pair = lax.optimization_barrier(jnp.sum(smooth_sign(pred[:, None] - pred[None, :]), axis=1))
        dpred = (live * (first - (1.0 - fair_eps) / (total * (total - 1)) * pair)).astype(jnp.bfloat16).astype(jnp.float32)
        dz = jnp.einsum('mcg,cj->mgj', dpred, w_prj)
        sig = jax.nn.sigmoid(pre)
        dpre = (dz * sig * (1.0 + pre * (1.0 - sig))).astype(jnp.bfloat16).astype(jnp.float32)
        sum_hidden = sum_hidden + jnp.einsum('mgi,mgj->ij', area, dpre)
        darea = jnp.einsum('mgj,ij->mgi', dpre, w_hid).astype(jnp.bfloat16).astype(jnp.float32)
        dext = jnp.einsum('gs,mgi->msi', counts, darea)
        sum_mesh = sum_mesh.at[:, below].add(dext[:, :MESH_DEV])
        sum_mesh = sum_mesh.at[:, tile].add(dext[:, MESH_DEV:2 * MESH_DEV])
        sum_mesh = sum_mesh.at[:, above].add(dext[:, 2 * MESH_DEV:])
        return ((sum_hidden, sum_mesh), None)
    start_carry = (jnp.zeros((L, L), jnp.float32), jnp.zeros((MEMBERS, N_SPACE, MESH_DEV, L), jnp.float32))
    final, unused = lax.scan(step, start_carry, jnp.arange(N_SPACE, dtype=jnp.int32))
    grad_hidden, grad_mesh = final
    return (grad_hidden, grad_mesh.reshape(MEMBERS, MESH, L).astype(jnp.bfloat16))
```

```python
import itertools

import jax
import jax.numpy as jnp
from jax import lax
from jax.sharding import Mesh
from jax.sharding import PartitionSpec as P

NAMES = ("xl", "c", "y", "z", "xh")
MEMBER = ("xl", "c")
SPACE = ("y", "z", "xh")
BF16 = jnp.bfloat16
F32 = jnp.float32

fair_eps = 0.05
smooth_sq = 0.01


def permute(value, axes, moved):
    sizes = [lax.axis_size(a) for a in axes]
    pairs = []
    for at in itertools.product(*[range(s) for s in sizes]):
        source = target = 0
        for size, a, b in zip(sizes, at, moved(*at)):
            source, target = source * size + a, target * size + b % size
        pairs.append((source, target))
    return lax.ppermute(value, axes if len(axes) > 1 else axes[0], pairs)


def shifted(value, axes, steps):
    count = lax.axis_size(axes)
    return lax.ppermute(value, axes, [(i, (i + steps) % count) for i in range(count)])


def piece(parts, at):
    return lax.dynamic_index_in_dim(parts, at, 0, keepdims=False)


def smooth_sign(value):
    return value / jnp.sqrt(value * value + smooth_sq)


def loss_grad(own, everyone, truth, live, total):
    values = own.astype(F32)
    first = smooth_sign(values - truth.astype(F32)[None]) / total
    pair = jnp.sum(smooth_sign(values[:, None] - everyone.astype(F32)[None]), axis=1)
    return (live * (first - (1.0 - fair_eps) / (total * (total - 1)) * pair)).astype(BF16)


def reduce_rows(grad):
    rows, cols = grad.shape
    n_y, n_z, n_x, n_l = (lax.axis_size(a) for a in ("y", "z", "xh", "xl"))
    c, y = lax.axis_index("c"), lax.axis_index("y")
    half = cols // 2
    left, right = grad[:, :half], grad[:, half:]
    keep = jnp.where(c == 0, left, right)
    give = jnp.where(c == 0, right, left)
    got = shifted(give, "c", 1)
    parts = (keep.astype(F32) + got.astype(F32)).astype(BF16).reshape(n_y, rows // n_y, half)
    steps = [s for s in range(1, n_y)]
    got = [shifted(piece(parts, (y + s) % n_y), "y", s) for s in steps]
    total = piece(parts, y).astype(F32)
    for g in got:
        total = total + g.astype(F32)
    own_rows = rows // (n_y * n_z * n_x)
    quarter = half // n_l
    parts = total.astype(BF16).reshape(n_z * n_x, own_rows, n_l, quarter).transpose(2, 0, 1, 3)
    parts = parts.reshape(n_l * n_z * n_x, own_rows, quarter)
    got = lax.all_to_all(parts, ("xl", "z", "xh"), 0, 0)
    mine = got.astype(F32).sum(0).astype(BF16)
    other = shifted(mine, "xl", 1)
    first = lax.axis_index("xl") == 0
    mine = jnp.concatenate([jnp.where(first, mine, other), jnp.where(first, other, mine)], axis=1)
    other = shifted(mine, "c", 1)
    return jnp.concatenate(
        [jnp.where(c == 0, mine, other), jnp.where(c == 0, other, mine)], axis=1
    ).astype(F32)


def shards(mesh_latent, w_hidden, w_out, target, slots, lengths):
    width = mesh_latent.shape[1]
    grid_rows = target.shape[1]
    total = mesh_latent.shape[0] * lax.axis_size(MEMBER)
    before = shifted(mesh_latent, SPACE, 1)
    after = shifted(mesh_latent, SPACE, -1)
    extended = jnp.concatenate([before, mesh_latent, after], axis=1)
    positions = jnp.arange(3 * width, dtype=jnp.int32)
    counts_f = jnp.zeros((grid_rows, 3 * width), F32)
    for k in range(3):
        counts_f = counts_f + (slots[k][:, None] == positions[None, :]).astype(F32)
    counts = counts_f.astype(BF16)
    area = jnp.einsum("gs,msl->mgl", counts, extended, preferred_element_type=F32).astype(BF16)
    pre = jnp.einsum("mgl,lj->mgj", area, w_hidden, preferred_element_type=F32)
    hidden = jax.nn.silu(pre).astype(BF16)
    pred = jnp.einsum("cj,mgj->mcg", w_out, hidden, preferred_element_type=F32).astype(BF16)
    live = (jnp.arange(grid_rows, dtype=jnp.int32) < lengths[0]).astype(F32)
    pair = jnp.concatenate([pred, shifted(pred, "xl", 1)], axis=0)
    everyone = jnp.concatenate([pair, shifted(pair, "c", 1)], axis=0)
    dpred = loss_grad(pred, everyone, target, live, total)
    dz = jnp.einsum("mcg,cj->mgj", dpred, w_out, preferred_element_type=F32)
    sig = jax.nn.sigmoid(pre)
    dpre = (dz * sig * (1.0 + pre * (1.0 - sig))).astype(BF16)
    grad = jnp.einsum("mgi,mgj->ij", area, dpre, preferred_element_type=F32).astype(BF16)
    grad_hidden = reduce_rows(grad)
    darea = jnp.einsum("mgj,ij->mgi", dpre, w_hidden, preferred_element_type=F32).astype(BF16)
    dext = jnp.einsum("gs,mgi->msi", counts, darea, preferred_element_type=F32)
    from_right = shifted(dext[:, :width].astype(BF16), SPACE, -1).astype(F32)
    from_left = shifted(dext[:, 2 * width :].astype(BF16), SPACE, 1).astype(F32)
    grad_mesh = (dext[:, width : 2 * width] + from_right + from_left).astype(BF16)
    return (grad_hidden, grad_mesh)


def solution(mesh):
    finer = Mesh(mesh.devices.reshape(2, 2, 4, 8, 2), NAMES)
    in_specs = (P(MEMBER, SPACE, None), P(), P(), P(None, SPACE), P(None, SPACE), P(SPACE))
    out_specs = (P(SPACE, None), P(MEMBER, SPACE, None))
    return jax.shard_map(
        shards, mesh=finer, in_specs=in_specs, out_specs=out_specs, check_vma=False
    )
```

```python
import functools
import itertools

import jax
import jax.numpy as jnp
from jax import lax
from jax.experimental import pallas as pl
from jax.experimental.pallas import tpu as pltpu
from jax.sharding import Mesh
from jax.sharding import PartitionSpec as P

NAMES = ("xl", "c", "y", "z", "xh")
MEMBER = ("xl", "c")
SPACE = ("y", "z", "xh")
BF16 = jnp.bfloat16
F32 = jnp.float32
VMEM = pl.BlockSpec(memory_space=pltpu.VMEM)
SMEM = pl.BlockSpec(memory_space=pltpu.SMEM)
grant = 16 << 20

fair_eps = 0.05
smooth_sq = 0.01
chunk = 256


def permute(value, axes, moved):
    sizes = [lax.axis_size(a) for a in axes]
    pairs = []
    for at in itertools.product(*[range(s) for s in sizes]):
        source = target = 0
        for size, a, b in zip(sizes, at, moved(*at)):
            source, target = source * size + a, target * size + b % size
        pairs.append((source, target))
    return lax.ppermute(value, axes if len(axes) > 1 else axes[0], pairs)


def shifted(value, axis, steps):
    return permute(value, (axis,), lambda i: (i + steps,))


def relayed(value, sign):
    n_y, n_z = lax.axis_size("y"), lax.axis_size("z")

    def moved(y, z, xh):
        k = (y * n_z + z + (sign if xh == 0 else -sign)) % (n_y * n_z)
        return (k // n_z, k % n_z, xh)

    return permute(value, SPACE, moved)


def call(kernel, out_shape, *args, scalars=0, final=False):
    on_chip = [pltpu.with_memory_space_constraint(a, pltpu.VMEM) for a in args[scalars:]]
    return pl.pallas_call(
        kernel,
        out_shape=[
            jax.ShapeDtypeStruct(*s) if final else pltpu.VMEM(*s) for s in out_shape
        ],
        in_specs=[SMEM] * scalars + [VMEM] * len(on_chip),
        out_specs=[VMEM] * len(out_shape),
        compiler_params=pltpu.CompilerParams(vmem_limit_bytes=grant),
    )(*args[:scalars], *on_chip)


def dot(a, b, ca=1, cb=0):
    return lax.dot_general(a, b, (((ca,), (cb,)), ((), ())), preferred_element_type=F32)


def stage_kernel(slots_ref, *refs):
    sources, (counts_ref, flipped_ref, *targets, sems) = refs[:3], refs[3:]
    copies = [
        pltpu.make_async_copy(a, b, sems.at[k]) for k, (a, b) in enumerate(zip(sources, targets))
    ]
    for copy in copies:
        copy.start()
    n, g = flipped_ref.shape
    xh = lax.axis_index("xh")
    at = lax.broadcasted_iota(jnp.int32, (n, g), 0)
    width = n // 3
    far = jnp.where(xh == 0, 0, 2 * width)
    near = jnp.where(xh == 0, 2 * width, 0)
    start = jnp.where(at < width, width, jnp.where(at < 2 * width, near - width, far - 2 * width))
    moved = at + start
    total = jnp.zeros((n, g), F32)
    for k in range(3):
        total = total + jnp.where(slots_ref[k : k + 1, :] == moved, 1.0, 0.0)
    flipped_ref[...] = total.astype(BF16)
    counts_ref[...] = total.T.astype(BF16)
    for copy in copies:
        copy.wait()


def staged(slots, sources, grid_rows, nodes):
    shapes = [((grid_rows, nodes), BF16), ((nodes, grid_rows), BF16)]
    shapes += [(a.shape, a.dtype) for a in sources]
    return pl.pallas_call(
        stage_kernel,
        out_shape=[pltpu.VMEM(shape, dtype) for shape, dtype in shapes],
        in_specs=[VMEM] + [pl.BlockSpec(memory_space=pl.ANY)] * len(sources),
        out_specs=[VMEM] * len(shapes),
        scratch_shapes=[pltpu.SemaphoreType.DMA((len(sources),))],
        compiler_params=pltpu.CompilerParams(vmem_limit_bytes=grant),
    )(slots, *sources)


def forward_kernel(counts_ref, own_ref, rec_ref, fwd_ref, w_ref, wo_ref, turned_ref, gate_ref, pred_ref):
    extended = jnp.concatenate([own_ref[...], rec_ref[...], fwd_ref[...]], axis=0)
    area = dot(counts_ref[...], extended).astype(BF16)
    turned_ref[...] = area.T
    total = None
    for n in range(0, w_ref.shape[1], chunk):
        pre = dot(area, w_ref[:, n : n + chunk])
        sig = 0.5 * jnp.tanh(0.5 * pre) + 0.5
        value = pre * sig
        gate_ref[:, n : n + chunk] = (sig * (1.0 + (pre - value))).astype(BF16)
        part = dot(wo_ref[:, n : n + chunk], value.astype(BF16), 1, 1)
        total = part if total is None else total + part
    pred_ref[...] = total.astype(BF16)


def smooth_sign(value):
    return value * lax.rsqrt(value * value + smooth_sq)


def half_slopes(start, half, wo_ref, gates, dps, slopes, turned, out):
    cols = pl.ds(pl.multiple_of(start, half), half)
    wo = wo_ref[:, cols]
    part = None
    for dp, gate, slope, area in zip(dps, gates, slopes, turned):
        value = (dot(dp[...], wo, 0, 0) * gate[:, cols].astype(F32)).astype(BF16)
        slope[...] = value
        more = dot(area[...], value)
        part = more if part is None else part + more
    out[...] = part.astype(out.dtype)


def give_kernel(total, len_ref, *refs):
    preds, (target_ref, wo_ref, t0, t1, gate0, gate1, dp0, dp1, s0, s1, out) = refs[:8], refs[8:]
    channels, _ = target_ref.shape
    scale = (1.0 - fair_eps) / (total * (total - 1))
    for r in range(0, channels, 16):
        rows = slice(r, min(r + 16, channels))
        own = [preds[0][rows].astype(F32), preds[1][rows].astype(F32)]
        truth = target_ref[rows].astype(F32)
        mutual = smooth_sign(own[0] - own[1])
        pairs = [mutual, -mutual]
        for ref in preds[2:]:
            other = ref[rows].astype(F32)
            pairs = [p + smooth_sign(v - other) for p, v in zip(pairs, own)]
        at = lax.broadcasted_iota(jnp.int32, truth.shape, 1)
        for ref, v, p in zip((dp0, dp1), own, pairs):
            value = smooth_sign(v - truth) * (1.0 / total) - scale * p
            ref[rows] = jnp.where(at < len_ref[0], value, 0.0).astype(BF16)
    half = out.shape[1]
    start = (1 - lax.axis_index("c")) * half
    half_slopes(start, half, wo_ref, (gate0, gate1), (dp0, dp1), (s0, s1), (t0, t1), out)


def keep_kernel(wo_ref, t0, t1, gate0, gate1, dp0, dp1, s0, s1, out):
    half = out.shape[1]
    start = lax.axis_index("c") * half
    half_slopes(start, half, wo_ref, (gate0, gate1), (dp0, dp1), (s0, s1), (t0, t1), out)


def cores_kernel(keep_ref, got_ref, own_ref, *outs):
    size = own_ref.shape[0]
    n_y = len(outs) + 1
    for s, out in enumerate((own_ref,) + outs):
        to = lax.rem(lax.axis_index("y") + s, n_y)
        rows = pl.ds(pl.multiple_of(to * size, size), size)
        out[...] = (keep_ref[rows, :].astype(F32) + got_ref[rows, :].astype(F32)).astype(out.dtype)


def total_kernel(first_ref, *refs):
    total = first_ref[...].astype(F32)
    for ref in refs[:-1]:
        total = total + ref[...].astype(F32)
    refs[-1][...] = total.astype(refs[-1].dtype)


def columns_kernel(parts_ref, mine_ref, theirs_ref):
    size = mine_ref.shape[0]
    xh = lax.axis_index("xh")
    total = parts_ref[0].astype(F32)
    for k in range(1, parts_ref.shape[0]):
        total = total + parts_ref[k].astype(F32)
    first, second = total[:size], total[size:]
    mine_ref[...] = jnp.where(xh == 0, first, second).astype(BF16)
    theirs_ref[...] = jnp.where(xh == 0, second, first).astype(BF16)


def place_kernel(mine_ref, other_ref, out_ref):
    half = mine_ref.shape[1]
    first = lax.axis_index("c") == 0
    mine, other = mine_ref[...].astype(F32), other_ref[...].astype(F32)
    out_ref[:, :half] = jnp.where(first, mine, other)
    out_ref[:, half:] = jnp.where(first, other, mine)


def backward_kernel(flipped_ref, w_ref, give_ref, keep_ref, own_ref, rec_ref, fwd_ref):
    half = give_ref.shape[1]
    width = own_ref.shape[0]
    c = lax.axis_index("c")
    give = pl.ds(pl.multiple_of((1 - c) * half, half), half)
    keep = pl.ds(pl.multiple_of(c * half, half), half)
    for n in range(0, w_ref.shape[0], chunk):
        rows = slice(n, n + chunk)
        darea = dot(give_ref[...], w_ref[rows, give], 1, 1) + dot(keep_ref[...], w_ref[rows, keep], 1, 1)
        dext = dot(flipped_ref[...], darea.astype(BF16))
        own_ref[:, rows] = dext[:width]
        rec_ref[:, rows] = dext[width : 2 * width]
        fwd_ref[:, rows] = dext[2 * width :].astype(BF16)


def step(mesh_latent, w_hidden, w_out, target, slots, lengths):
    members, width, wide = mesh_latent.shape
    channels, grid_rows = target.shape
    total = members * lax.axis_size(MEMBER)
    half = wide // 2
    n_y, n_z, n_x = (lax.axis_size(a) for a in SPACE)

    own = [mesh_latent[m] for m in range(members)]
    rec = []
    for v in own:
        rec.append(shifted(v, "xh", 1))
    fwd = [relayed(v, 1) for v in rec]
    counts, flipped, w_hidden, w_out, target = staged(
        slots, (w_hidden, w_out, target), grid_rows, 3 * width
    )
    area, gate, pred = [], [], []
    for m in range(members):
        a, p, q = call(
            forward_kernel,
            [((wide, grid_rows), BF16), ((grid_rows, wide), BF16), ((channels, grid_rows), BF16)],
            counts, own[m], rec[m], fwd[m], w_hidden, w_out,
        )
        area.append(a)
        gate.append(p)
        pred.append(q)
    others = []
    for q in pred:
        others += [
            shifted(q, "xl", 1), permute(q, MEMBER, lambda a, b: (1 - a, 1 - b)), shifted(q, "c", 1)
        ]

    slope = ((grid_rows, half), BF16)
    part = ((wide, half), BF16)
    dp = ((channels, grid_rows), BF16)
    dp0, dp1, g0, g1, give = call(
        functools.partial(give_kernel, total), [dp, dp, slope, slope, part],
        lengths, *pred, *others, target, w_out, *area, *gate, scalars=1,
    )
    got = shifted(give, "c", 1)
    k0, k1, keep = call(keep_kernel, [slope, slope, part], w_out, *area, *gate, dp0, dp1)
    rows_y = (wide // n_y, half)
    mine, *give = call(cores_kernel, [(rows_y, F32)] + [(rows_y, BF16)] * (n_y - 1), keep, got)
    got = []
    for s, g in enumerate(give):
        got.append(shifted(g, "y", s + 1))

    node = ((width, wide), F32)
    back = []
    for g, k in ((g0, k0), (g1, k1)):
        back.append(
            call(backward_kernel, [node, node, ((width, wide), BF16)], flipped, w_hidden, g, k)
        )
    far = [relayed(b[2], -1) for b in back]
    far = [call(total_kernel, [((width, wide), BF16)], b[1], f)[0] for b, f in zip(back, far)]

    (rows,) = call(total_kernel, [(rows_y, BF16)], mine, *got)
    rows, far[0] = lax.optimization_barrier((rows, far[0]))
    far = [shifted(f, "xh", 1) for f in far]
    rows = lax.all_to_all(rows.reshape(n_z, wide // (n_y * n_z), half), "z", 0, 0)
    out_rows = (wide // (n_y * n_z * n_x), half)
    mine, theirs = call(columns_kernel, [(out_rows, BF16)] * 2, rows)
    (mine,) = call(
        total_kernel, [(out_rows, BF16)],
        mine, shifted(mine, "xl", 1), shifted(theirs, "xh", 1),
        permute(theirs, ("xl", "xh"), lambda a, b: (1 - a, 1 - b)),
    )
    (grad_hidden,) = call(place_kernel, [((out_rows[0], wide), F32)], mine, shifted(mine, "c", 1), final=True)
    grad_mesh = jnp.stack([(b[0] + f.astype(F32)).astype(BF16) for b, f in zip(back, far)])
    return (grad_hidden, grad_mesh)


def solution(mesh):
    finer = Mesh(mesh.devices.reshape(2, 2, 4, 8, 2), NAMES)
    in_specs = (P(MEMBER, SPACE, None), P(), P(), P(None, SPACE), P(None, SPACE), P(SPACE))
    out_specs = (P(SPACE, None), P(MEMBER, SPACE, None))
    return jax.shard_map(step, mesh=finer, in_specs=in_specs, out_specs=out_specs, check_vma=False)
```

```python
import functools
import itertools

import jax
import jax.numpy as jnp
from jax import lax
from jax.experimental import pallas as pl
from jax.experimental.pallas import tpu as pltpu
from jax.sharding import Mesh
from jax.sharding import PartitionSpec as P

NAMES = ("xl", "c", "y", "z", "xh")
MEMBER = ("xl", "c")
SPACE = ("y", "z", "xh")
BF16 = jnp.bfloat16
F32 = jnp.float32
VMEM = pl.BlockSpec(memory_space=pltpu.VMEM)
SMEM = pl.BlockSpec(memory_space=pltpu.SMEM)
grant = 16 << 20

fair_eps = 0.05
smooth_sq = 0.01
chunk = 256


def permute(value, axes, moved):
    sizes = [lax.axis_size(a) for a in axes]
    pairs = []
    for at in itertools.product(*[range(s) for s in sizes]):
        source = target = 0
        for size, a, b in zip(sizes, at, moved(*at)):
            source, target = source * size + a, target * size + b % size
        pairs.append((source, target))
    return lax.ppermute(value, axes if len(axes) > 1 else axes[0], pairs)


def shifted(value, axis, steps):
    return permute(value, (axis,), lambda i: (i + steps,))


def relayed(value, sign):
    n_y, n_z = lax.axis_size("y"), lax.axis_size("z")

    def moved(y, z, xh):
        k = (y * n_z + z + (sign if xh == 0 else -sign)) % (n_y * n_z)
        return (k // n_z, k % n_z, xh)

    return permute(value, SPACE, moved)


def call(kernel, out_shape, *args, scalars=0, final=False):
    on_chip = [pltpu.with_memory_space_constraint(a, pltpu.VMEM) for a in args[scalars:]]
    return pl.pallas_call(
        kernel,
        out_shape=[
            jax.ShapeDtypeStruct(*s) if final else pltpu.VMEM(*s) for s in out_shape
        ],
        in_specs=[SMEM] * scalars + [VMEM] * len(on_chip),
        out_specs=[VMEM] * len(out_shape),
        compiler_params=pltpu.CompilerParams(vmem_limit_bytes=grant),
    )(*args[:scalars], *on_chip)


def dot(a, b, ca=1, cb=0):
    return lax.dot_general(a, b, (((ca,), (cb,)), ((), ())), preferred_element_type=F32)


def stage_kernel(slots_ref, *refs):
    sources, (counts_ref, flipped_ref, *targets, sems) = refs[:3], refs[3:]
    copies = [
        pltpu.make_async_copy(a, b, sems.at[k]) for k, (a, b) in enumerate(zip(sources, targets))
    ]
    for copy in copies:
        copy.start()
    n, g = flipped_ref.shape
    xh = lax.axis_index("xh")
    at = lax.broadcasted_iota(jnp.int32, (n, g), 0)
    width = n // 3
    far = jnp.where(xh == 0, 0, 2 * width)
    near = jnp.where(xh == 0, 2 * width, 0)
    start = jnp.where(at < width, width, jnp.where(at < 2 * width, near - width, far - 2 * width))
    moved = at + start
    total = jnp.zeros((n, g), F32)
    for k in range(3):
        total = total + jnp.where(slots_ref[k : k + 1, :] == moved, 1.0, 0.0)
    flipped_ref[...] = total.astype(BF16)
    counts_ref[...] = total.T.astype(BF16)
    for copy in copies:
        copy.wait()


def staged(slots, sources, grid_rows, nodes):
    shapes = [((grid_rows, nodes), BF16), ((nodes, grid_rows), BF16)]
    shapes += [(a.shape, a.dtype) for a in sources]
    return pl.pallas_call(
        stage_kernel,
        out_shape=[pltpu.VMEM(shape, dtype) for shape, dtype in shapes],
        in_specs=[VMEM] + [pl.BlockSpec(memory_space=pl.ANY)] * len(sources),
        out_specs=[VMEM] * len(shapes),
        scratch_shapes=[pltpu.SemaphoreType.DMA((len(sources),))],
        compiler_params=pltpu.CompilerParams(vmem_limit_bytes=grant),
    )(slots, *sources)


def forward_kernel(counts_ref, own_ref, rec_ref, fwd_ref, w_ref, wo_ref, turned_ref, gate_ref, pred_ref):
    extended = jnp.concatenate([own_ref[...], rec_ref[...], fwd_ref[...]], axis=0)
    area = dot(counts_ref[...], extended).astype(BF16)
    turned_ref[...] = area.T
    total = None
    for n in range(0, w_ref.shape[1], chunk):
        pre = dot(area, w_ref[:, n : n + chunk])
        sig = 0.5 * jnp.tanh(0.5 * pre) + 0.5
        value = pre * sig
        gate_ref[:, n : n + chunk] = (sig * (1.0 + (pre - value))).astype(BF16)
        part = dot(wo_ref[:, n : n + chunk], value.astype(BF16), 1, 1)
        total = part if total is None else total + part
    pred_ref[...] = total.astype(BF16)


def smooth_sign(value):
    return value * lax.rsqrt(value * value + smooth_sq)


def half_slopes(start, half, wo_ref, gates, dps, slopes, turned, out):
    cols = pl.ds(pl.multiple_of(start, half), half)
    wo = wo_ref[:, cols]
    part = None
    for dp, gate, slope, area in zip(dps, gates, slopes, turned):
        value = (dot(dp[...], wo, 0, 0) * gate[:, cols].astype(F32)).astype(BF16)
        slope[...] = value
        more = dot(area[...], value)
        part = more if part is None else part + more
    out[...] = part.astype(out.dtype).reshape(out.shape)


def give_kernel(total, len_ref, *refs):
    preds, (target_ref, wo_ref, t0, t1, gate0, gate1, dp0, dp1, s0, s1, out) = refs[:8], refs[8:]
    channels, _ = target_ref.shape
    scale = (1.0 - fair_eps) / (total * (total - 1))
    for r in range(0, channels, 16):
        rows = slice(r, min(r + 16, channels))
        own = [preds[0][rows].astype(F32), preds[1][rows].astype(F32)]
        truth = target_ref[rows].astype(F32)
        mutual = smooth_sign(own[0] - own[1])
        pairs = [mutual, -mutual]
        for ref in preds[2:]:
            other = ref[rows].astype(F32)
            pairs = [p + smooth_sign(v - other) for p, v in zip(pairs, own)]
        at = lax.broadcasted_iota(jnp.int32, truth.shape, 1)
        for ref, v, p in zip((dp0, dp1), own, pairs):
            value = smooth_sign(v - truth) * (1.0 / total) - scale * p
            ref[rows] = jnp.where(at < len_ref[0], value, 0.0).astype(BF16)
    half = out.shape[-1]
    start = (1 - lax.axis_index("c")) * half
    half_slopes(start, half, wo_ref, (gate0, gate1), (dp0, dp1), (s0, s1), (t0, t1), out)


def keep_kernel(wo_ref, t0, t1, gate0, gate1, dp0, dp1, s0, s1, out):
    half = out.shape[-1]
    start = lax.axis_index("c") * half
    half_slopes(start, half, wo_ref, (gate0, gate1), (dp0, dp1), (s0, s1), (t0, t1), out)


def cores_kernel(keep_ref, got_ref, own_ref, *outs):
    wide = own_ref.shape[-1]
    for out, (a, b) in zip((own_ref,) + outs, ((0, 0), (0, 1), (1, 0), (1, 1))):
        xh = lax.rem(lax.axis_index("xh") + a, 2)
        xl = lax.rem(lax.axis_index("xl") + b, 2)
        cols = pl.ds(pl.multiple_of(xl * wide, wide), wide)
        out[...] = (
            keep_ref[:, xh, :, cols].astype(F32) + got_ref[:, xh, :, cols].astype(F32)
        ).astype(out.dtype)


def cut_kernel(first_ref, second_ref, third_ref, fourth_ref, own_ref, *outs):
    size = own_ref.shape[0]
    n_y = len(outs) + 1
    for s, out in enumerate((own_ref,) + outs):
        to = lax.rem(lax.axis_index("y") + s, n_y)
        at = pl.ds(to * size, size)
        total = first_ref[at]
        for ref in (second_ref, third_ref, fourth_ref):
            total = total + ref[at].astype(F32)
        out[...] = total.astype(out.dtype)


def total_kernel(first_ref, *refs):
    total = first_ref[...].astype(F32)
    for ref in refs[:-1]:
        total = total + ref[...].astype(F32)
    refs[-1][...] = total.astype(refs[-1].dtype)


def sum_kernel(parts_ref, out_ref):
    total = parts_ref[0].astype(F32)
    for k in range(1, parts_ref.shape[0]):
        total = total + parts_ref[k].astype(F32)
    out_ref[...] = total.astype(out_ref.dtype)


def place_kernel(mine_ref, x_ref, c_ref, both_ref, out_ref):
    wide = mine_ref.shape[1]
    c, xl = lax.axis_index("c"), lax.axis_index("xl")
    for k, ref in enumerate((mine_ref, x_ref, c_ref, both_ref)):
        at = lax.rem(c + k // 2, 2) * 2 + lax.rem(xl + k, 2)
        cols = pl.ds(pl.multiple_of(at * wide, wide), wide)
        out_ref[:, cols] = ref[...].astype(F32)


def nodes_kernel(own0_ref, own1_ref, far0_ref, far1_ref, out_ref):
    out_ref[0] = (own0_ref[...] + far0_ref[...].astype(F32)).astype(BF16)
    out_ref[1] = (own1_ref[...] + far1_ref[...].astype(F32)).astype(BF16)


def backward_kernel(flipped_ref, w_ref, give_ref, keep_ref, own_ref, rec_ref, fwd_ref):
    half = give_ref.shape[1]
    width = own_ref.shape[0]
    c = lax.axis_index("c")
    give = pl.ds(pl.multiple_of((1 - c) * half, half), half)
    keep = pl.ds(pl.multiple_of(c * half, half), half)
    for n in range(0, w_ref.shape[0], chunk):
        rows = slice(n, n + chunk)
        darea = dot(give_ref[...], w_ref[rows, give], 1, 1) + dot(keep_ref[...], w_ref[rows, keep], 1, 1)
        dext = dot(flipped_ref[...], darea.astype(BF16))
        own_ref[:, rows] = dext[:width]
        rec_ref[:, rows] = dext[width : 2 * width]
        fwd_ref[:, rows] = dext[2 * width :].astype(BF16)


def step(mesh_latent, w_hidden, w_out, target, slots, lengths):
    members, width, wide = mesh_latent.shape
    channels, grid_rows = target.shape
    total = members * lax.axis_size(MEMBER)
    half = wide // 2
    n_y, n_z, n_x = (lax.axis_size(a) for a in SPACE)

    own = [mesh_latent[m] for m in range(members)]
    rec = []
    for v in own:
        rec.append(shifted(v, "xh", 1))
    fwd = [relayed(v, 1) for v in rec]
    counts, flipped, w_hidden, w_out, target = staged(
        slots, (w_hidden, w_out, target), grid_rows, 3 * width
    )
    area, gate, pred = [], [], []
    for m in range(members):
        a, p, q = call(
            forward_kernel,
            [((wide, grid_rows), BF16), ((grid_rows, wide), BF16), ((channels, grid_rows), BF16)],
            counts, own[m], rec[m], fwd[m], w_hidden, w_out,
        )
        area.append(a)
        gate.append(p)
        pred.append(q)
    others = []
    for q in pred:
        others += [
            shifted(q, "xl", 1), permute(q, MEMBER, lambda a, b: (1 - a, 1 - b)), shifted(q, "c", 1)
        ]

    slope = ((grid_rows, half), BF16)
    out_rows = wide // (n_y * n_z * n_x)
    part = ((n_y * n_z, n_x, out_rows, half), BF16)
    dp = ((channels, grid_rows), BF16)
    dp0, dp1, g0, g1, give = call(
        functools.partial(give_kernel, total), [dp, dp, slope, slope, part],
        lengths, *pred, *others, target, w_out, *area, *gate, scalars=1,
    )
    got = shifted(give, "c", 1)
    k0, k1, keep = call(keep_kernel, [slope, slope, part], w_out, *area, *gate, dp0, dp1)
    part = ((n_y * n_z, out_rows, half // 2), BF16)
    mine, *give = call(cores_kernel, [(part[0], F32)] + [part] * 3, keep, got)
    got = []
    for axes, g in zip((("xl",), ("xh",), ("xl", "xh")), give):
        got.append(permute(g, axes, lambda *at: tuple(1 - i for i in at)))
    part = ((n_z, out_rows, half // 2), BF16)
    mine, *give = call(cut_kernel, [(part[0], F32)] + [part] * (n_y - 1), mine, *got)
    got = []
    for s in (2, 1, 3):
        got.append(shifted(give[s - 1], "y", s))
    (rows,) = call(total_kernel, [part], mine, *got)

    node = ((width, wide), F32)
    back = []
    for g, k in ((g0, k0), (g1, k1)):
        back.append(
            call(backward_kernel, [node, node, ((width, wide), BF16)], flipped, w_hidden, g, k)
        )
    far = []
    for b in back:
        moved = relayed(b[2], -1)
        far.append(call(total_kernel, [((width, wide), BF16)], b[1], moved)[0])

    for m in range(members):
        far[m] = shifted(far[m], "xh", 1)
    rows = lax.all_to_all(rows, "z", 0, 0)
    (mine,) = call(sum_kernel, [((out_rows, half // 2), BF16)], rows)
    (grad_hidden,) = call(
        place_kernel, [((out_rows, wide), F32)],
        mine, shifted(mine, "xl", 1), shifted(mine, "c", 1),
        permute(mine, MEMBER, lambda a, b: (1 - a, 1 - b)), final=True,
    )
    (grad_mesh,) = call(
        nodes_kernel, [((members, width, wide), BF16)], *[b[0] for b in back], *far, final=True
    )
    return (grad_hidden, grad_mesh)


def solution(mesh):
    finer = Mesh(mesh.devices.reshape(2, 2, 4, 8, 2), NAMES)
    in_specs = (P(MEMBER, SPACE, None), P(), P(), P(None, SPACE), P(None, SPACE), P(SPACE))
    out_specs = (P(SPACE, None), P(MEMBER, SPACE, None))
    return jax.shard_map(step, mesh=finer, in_specs=in_specs, out_specs=out_specs, check_vma=False)
```

```python
import functools
import itertools

import jax
import jax.numpy as jnp
from jax import lax
from jax.experimental import pallas as pl
from jax.experimental.pallas import tpu as pltpu
from jax.sharding import Mesh
from jax.sharding import PartitionSpec as P

NAMES = ("xl", "c", "y", "z", "xh")
MEMBER = ("xl", "c")
SPACE = ("y", "z", "xh")
BF16 = jnp.bfloat16
F32 = jnp.float32
VMEM = pl.BlockSpec(memory_space=pltpu.VMEM)
SMEM = pl.BlockSpec(memory_space=pltpu.SMEM)
grant = 16 << 20

fair_eps = 0.05
smooth_sq = 0.01
chunk = 256


def permute(value, axes, moved):
    sizes = [lax.axis_size(a) for a in axes]
    pairs = []
    for at in itertools.product(*[range(s) for s in sizes]):
        source = target = 0
        for size, a, b in zip(sizes, at, moved(*at)):
            source, target = source * size + a, target * size + b % size
        pairs.append((source, target))
    return lax.ppermute(value, axes if len(axes) > 1 else axes[0], pairs)


def shifted(value, axis, steps):
    return permute(value, (axis,), lambda i: (i + steps,))


def relayed(value, sign):
    n_y, n_z = lax.axis_size("y"), lax.axis_size("z")

    def moved(y, z, xh):
        k = (y * n_z + z + (sign if xh == 0 else -sign)) % (n_y * n_z)
        return (k // n_z, k % n_z, xh)

    return permute(value, SPACE, moved)


def call(kernel, out_shape, *args, scalars=0, final=False):
    on_chip = [pltpu.with_memory_space_constraint(a, pltpu.VMEM) for a in args[scalars:]]
    return pl.pallas_call(
        kernel,
        out_shape=[
            jax.ShapeDtypeStruct(*s) if final else pltpu.VMEM(*s) for s in out_shape
        ],
        in_specs=[SMEM] * scalars + [VMEM] * len(on_chip),
        out_specs=[VMEM] * len(out_shape),
        compiler_params=pltpu.CompilerParams(vmem_limit_bytes=grant),
    )(*args[:scalars], *on_chip)


def dot(a, b, ca=1, cb=0):
    return lax.dot_general(a, b, (((ca,), (cb,)), ((), ())), preferred_element_type=F32)


def stage_kernel(slots_ref, *refs):
    sources, (counts_ref, flipped_ref, *targets, sems) = refs[:3], refs[3:]
    copies = [
        pltpu.make_async_copy(a, b, sems.at[k]) for k, (a, b) in enumerate(zip(sources, targets))
    ]
    for copy in copies:
        copy.start()
    n, g = flipped_ref.shape
    xh = lax.axis_index("xh")
    at = lax.broadcasted_iota(jnp.int32, (n, g), 0)
    width = n // 3
    far = jnp.where(xh == 0, 0, 2 * width)
    near = jnp.where(xh == 0, 2 * width, 0)
    start = jnp.where(at < width, width, jnp.where(at < 2 * width, near - width, far - 2 * width))
    moved = at + start
    total = jnp.zeros((n, g), F32)
    for k in range(3):
        total = total + jnp.where(slots_ref[k : k + 1, :] == moved, 1.0, 0.0)
    flipped_ref[...] = total.astype(BF16)
    counts_ref[...] = total.T.astype(BF16)
    for copy in copies:
        copy.wait()


def staged(slots, sources, grid_rows, nodes):
    shapes = [((grid_rows, nodes), BF16), ((nodes, grid_rows), BF16)]
    shapes += [(a.shape, a.dtype) for a in sources]
    return pl.pallas_call(
        stage_kernel,
        out_shape=[pltpu.VMEM(shape, dtype) for shape, dtype in shapes],
        in_specs=[VMEM] + [pl.BlockSpec(memory_space=pl.ANY)] * len(sources),
        out_specs=[VMEM] * len(shapes),
        scratch_shapes=[pltpu.SemaphoreType.DMA((len(sources),))],
        compiler_params=pltpu.CompilerParams(vmem_limit_bytes=grant),
    )(slots, *sources)


def forward_kernel(counts_ref, own_ref, rec_ref, fwd_ref, w_ref, wo_ref, turned_ref, gate_ref, pred_ref):
    extended = jnp.concatenate([own_ref[...], rec_ref[...], fwd_ref[...]], axis=0)
    area = dot(counts_ref[...], extended).astype(BF16)
    turned_ref[...] = area.T
    hidden = []
    for n in range(0, w_ref.shape[1], 2 * chunk):
        cols = slice(n, n + 2 * chunk)
        pre = dot(area, w_ref[:, cols])
        sig = 0.5 * jnp.tanh(0.5 * pre) + 0.5
        value = pre * sig
        gate_ref[:, cols] = (sig * (1.0 + (pre - value))).astype(BF16)
        hidden.append(value.astype(BF16))
    pred_ref[...] = dot(wo_ref[...], jnp.concatenate(hidden, axis=1), 1, 1).astype(BF16)


def smooth_sign(value):
    return value * lax.rsqrt(value * value + smooth_sq)


def half_slopes(start, half, wo_ref, gates, dps, slopes, turned, out):
    cols = pl.ds(pl.multiple_of(start, half), half)
    wo = wo_ref[:, cols]
    part = None
    for dp, gate, slope, area in zip(dps, gates, slopes, turned):
        value = (dot(dp[...], wo, 0, 0) * gate[:, cols].astype(F32)).astype(BF16)
        slope[...] = value
        more = dot(area[...], value)
        part = more if part is None else part + more
    out[...] = part.astype(out.dtype).reshape(out.shape)


def give_kernel(total, len_ref, *refs):
    preds, (target_ref, wo_ref, t0, t1, gate0, gate1, dp0, dp1, s0, s1, out) = refs[:8], refs[8:]
    channels, _ = target_ref.shape
    scale = (1.0 - fair_eps) / (total * (total - 1))
    for r in range(0, channels, 16):
        rows = slice(r, min(r + 16, channels))
        own = [preds[0][rows].astype(F32), preds[1][rows].astype(F32)]
        truth = target_ref[rows].astype(F32)
        mutual = smooth_sign(own[0] - own[1])
        pairs = [mutual, -mutual]
        for ref in preds[2:]:
            other = ref[rows].astype(F32)
            pairs = [p + smooth_sign(v - other) for p, v in zip(pairs, own)]
        at = lax.broadcasted_iota(jnp.int32, truth.shape, 1)
        for ref, v, p in zip((dp0, dp1), own, pairs):
            value = smooth_sign(v - truth) * (1.0 / total) - scale * p
            ref[rows] = jnp.where(at < len_ref[0], value, 0.0).astype(BF16)
    half = out.shape[-1]
    start = (1 - lax.axis_index("c")) * half
    half_slopes(start, half, wo_ref, (gate0, gate1), (dp0, dp1), (s0, s1), (t0, t1), out)


def keep_kernel(wo_ref, t0, t1, gate0, gate1, dp0, dp1, s0, s1, out):
    half = out.shape[-1]
    start = lax.axis_index("c") * half
    half_slopes(start, half, wo_ref, (gate0, gate1), (dp0, dp1), (s0, s1), (t0, t1), out)


def cores_kernel(keep_ref, got_ref, own_ref, *outs):
    wide = own_ref.shape[-1]
    for out, (a, b) in zip((own_ref,) + outs, ((0, 0), (0, 1), (1, 0), (1, 1))):
        xh = lax.rem(lax.axis_index("xh") + a, 2)
        xl = lax.rem(lax.axis_index("xl") + b, 2)
        cols = pl.ds(pl.multiple_of(xl * wide, wide), wide)
        out[...] = (
            keep_ref[:, xh, :, cols].astype(F32) + got_ref[:, xh, :, cols].astype(F32)
        ).astype(out.dtype)


def cut_kernel(first_ref, second_ref, third_ref, fourth_ref, own_ref, *outs):
    size = own_ref.shape[0]
    n_y = len(outs) + 1
    for s, out in enumerate((own_ref,) + outs):
        to = lax.rem(lax.axis_index("y") + s, n_y)
        at = pl.ds(to * size, size)
        total = first_ref[at]
        for ref in (second_ref, third_ref, fourth_ref):
            total = total + ref[at].astype(F32)
        out[...] = total.astype(out.dtype)


def total_kernel(first_ref, *refs):
    total = first_ref[...].astype(F32)
    for ref in refs[:-1]:
        total = total + ref[...].astype(F32)
    refs[-1][...] = total.astype(refs[-1].dtype)


def sum_kernel(parts_ref, out_ref):
    total = parts_ref[0].astype(F32)
    for k in range(1, parts_ref.shape[0]):
        total = total + parts_ref[k].astype(F32)
    out_ref[...] = total.astype(out_ref.dtype)


def place_kernel(mine_ref, x_ref, c_ref, both_ref, out_ref):
    wide = mine_ref.shape[1]
    c, xl = lax.axis_index("c"), lax.axis_index("xl")
    for k, ref in enumerate((mine_ref, x_ref, c_ref, both_ref)):
        at = lax.rem(c + k // 2, 2) * 2 + lax.rem(xl + k, 2)
        cols = pl.ds(pl.multiple_of(at * wide, wide), wide)
        out_ref[:, cols] = ref[...].astype(F32)


def join_kernel(rec0_ref, rec1_ref, far0_ref, far1_ref, out_ref):
    out_ref[0] = (rec0_ref[...] + far0_ref[...].astype(F32)).astype(BF16)
    out_ref[1] = (rec1_ref[...] + far1_ref[...].astype(F32)).astype(BF16)


def nodes_kernel(own0_ref, own1_ref, far_ref, out_ref):
    out_ref[0] = (own0_ref[...] + far_ref[0].astype(F32)).astype(BF16)
    out_ref[1] = (own1_ref[...] + far_ref[1].astype(F32)).astype(BF16)


def backward_kernel(flipped_ref, w_ref, give_ref, keep_ref, own_ref, rec_ref, fwd_ref):
    half = give_ref.shape[1]
    width = own_ref.shape[0]
    c = lax.axis_index("c")
    give = pl.ds(pl.multiple_of((1 - c) * half, half), half)
    keep = pl.ds(pl.multiple_of(c * half, half), half)
    for n in range(0, w_ref.shape[0], chunk):
        rows = slice(n, n + chunk)
        darea = dot(give_ref[...], w_ref[rows, give], 1, 1) + dot(keep_ref[...], w_ref[rows, keep], 1, 1)
        dext = dot(flipped_ref[...], darea.astype(BF16))
        own_ref[:, rows] = dext[:width]
        rec_ref[:, rows] = dext[width : 2 * width]
        fwd_ref[:, rows] = dext[2 * width :].astype(BF16)


def step(mesh_latent, w_hidden, w_out, target, slots, lengths):
    members, width, wide = mesh_latent.shape
    channels, grid_rows = target.shape
    total = members * lax.axis_size(MEMBER)
    half = wide // 2
    n_y, n_z, n_x = (lax.axis_size(a) for a in SPACE)

    own = [mesh_latent[m] for m in range(members)]
    rec = []
    for v in own:
        rec.append(shifted(v, "xh", 1))
    fwd = [relayed(v, 1) for v in rec]
    counts, flipped, w_hidden, w_out, target = staged(
        slots, (w_hidden, w_out, target), grid_rows, 3 * width
    )
    area, gate, pred = [], [], []
    for m in range(members):
        a, p, q = call(
            forward_kernel,
            [((wide, grid_rows), BF16), ((grid_rows, wide), BF16), ((channels, grid_rows), BF16)],
            counts, own[m], rec[m], fwd[m], w_hidden, w_out,
        )
        area.append(a)
        gate.append(p)
        pred.append(q)
    near, mate, last = [], [], []
    for m, q in enumerate(pred):
        near.append(shifted(q, "xl", 1))
        mate.append(shifted(q, "c", 1))
        last.append(shifted(near[m], "c", 1))
    others = near + mate + last

    slope = ((grid_rows, half), BF16)
    out_rows = wide // (n_y * n_z * n_x)
    part = ((n_y * n_z, n_x, out_rows, half), BF16)
    dp = ((channels, grid_rows), BF16)
    dp0, dp1, g0, g1, give = call(
        functools.partial(give_kernel, total), [dp, dp, slope, slope, part],
        lengths, *pred, *others, target, w_out, *area, *gate, scalars=1,
    )
    got = shifted(give, "c", 1)
    k0, k1, keep = call(keep_kernel, [slope, slope, part], w_out, *area, *gate, dp0, dp1)
    part = ((n_y * n_z, out_rows, half // 2), BF16)
    mine, *give = call(cores_kernel, [(part[0], F32)] + [part] * 3, keep, got)
    got = []
    for axes, g in zip((("xl",), ("xh",), ("xl", "xh")), give):
        got.append(permute(g, axes, lambda *at: tuple(1 - i for i in at)))
    part = ((n_z, out_rows, half // 2), BF16)
    mine, *give = call(cut_kernel, [(part[0], F32)] + [part] * (n_y - 1), mine, *got)
    got = []
    for s in (2, 1, 3):
        got.append(shifted(give[s - 1], "y", s))
    (rows,) = call(total_kernel, [part], mine, *got)

    node = ((width, wide), F32)
    back = []
    for g, k in ((g0, k0), (g1, k1)):
        back.append(
            call(backward_kernel, [node, node, ((width, wide), BF16)], flipped, w_hidden, g, k)
        )
    far = []
    for b in back:
        far.append(relayed(b[2], -1))
    (far,) = call(join_kernel, [((members, width, wide), BF16)], *[b[1] for b in back], *far)
    far = shifted(far, "xh", 1)
    rows = lax.all_to_all(rows, "z", 0, 0)
    (mine,) = call(sum_kernel, [((out_rows, half // 2), BF16)], rows)
    (grad_hidden,) = call(
        place_kernel, [((out_rows, wide), F32)],
        mine, shifted(mine, "xl", 1), shifted(mine, "c", 1),
        permute(mine, MEMBER, lambda a, b: (1 - a, 1 - b)), final=True,
    )
    (grad_mesh,) = call(
        nodes_kernel, [((members, width, wide), BF16)], *[b[0] for b in back], far, final=True
    )
    return (grad_hidden, grad_mesh)


def solution(mesh):
    finer = Mesh(mesh.devices.reshape(2, 2, 4, 8, 2), NAMES)
    in_specs = (P(MEMBER, SPACE, None), P(), P(), P(None, SPACE), P(None, SPACE), P(SPACE))
    out_specs = (P(SPACE, None), P(MEMBER, SPACE, None))
    return jax.shard_map(step, mesh=finer, in_specs=in_specs, out_specs=out_specs, check_vma=False)
```

```python
import functools
import itertools

import jax
import jax.numpy as jnp
from jax import lax
from jax.experimental import pallas as pl
from jax.experimental.pallas import tpu as pltpu
from jax.sharding import Mesh
from jax.sharding import PartitionSpec as P

NAMES = ("xl", "c", "y", "z", "xh")
MEMBER = ("xl", "c")
SPACE = ("y", "z", "xh")
BF16 = jnp.bfloat16
F32 = jnp.float32
VMEM = pl.BlockSpec(memory_space=pltpu.VMEM)
SMEM = pl.BlockSpec(memory_space=pltpu.SMEM)
grant = 16 << 20

fair_eps = 0.05
smooth_sq = 0.01
chunk = 256


def permute(value, axes, moved):
    sizes = [lax.axis_size(a) for a in axes]
    pairs = []
    for at in itertools.product(*[range(s) for s in sizes]):
        source = target = 0
        for size, a, b in zip(sizes, at, moved(*at)):
            source, target = source * size + a, target * size + b % size
        pairs.append((source, target))
    return lax.ppermute(value, axes if len(axes) > 1 else axes[0], pairs)


def shifted(value, axis, steps):
    return permute(value, (axis,), lambda i: (i + steps,))


def relayed(value, sign):
    n_y, n_z = lax.axis_size("y"), lax.axis_size("z")

    def moved(y, z, xh):
        k = (y * n_z + z + (sign if xh == 0 else -sign)) % (n_y * n_z)
        return (k // n_z, k % n_z, xh)

    return permute(value, SPACE, moved)


def call(kernel, out_shape, *args, scalars=0, final=False):
    on_chip = [pltpu.with_memory_space_constraint(a, pltpu.VMEM) for a in args[scalars:]]
    return pl.pallas_call(
        kernel,
        out_shape=[
            jax.ShapeDtypeStruct(*s) if final else pltpu.VMEM(*s) for s in out_shape
        ],
        in_specs=[SMEM] * scalars + [VMEM] * len(on_chip),
        out_specs=[VMEM] * len(out_shape),
        compiler_params=pltpu.CompilerParams(vmem_limit_bytes=grant),
    )(*args[:scalars], *on_chip)


def dot(a, b, ca=1, cb=0):
    return lax.dot_general(a, b, (((ca,), (cb,)), ((), ())), preferred_element_type=F32)


def stage_kernel(slots_ref, *refs):
    sources, (counts_ref, flipped_ref, *targets, sems) = refs[:3], refs[3:]
    copies = [
        pltpu.make_async_copy(a, b, sems.at[k]) for k, (a, b) in enumerate(zip(sources, targets))
    ]
    for copy in copies:
        copy.start()
    n, g = flipped_ref.shape
    xh = lax.axis_index("xh")
    at = lax.broadcasted_iota(jnp.int32, (n, g), 0)
    width = n // 3
    far = jnp.where(xh == 0, 0, 2 * width)
    near = jnp.where(xh == 0, 2 * width, 0)
    start = jnp.where(at < width, width, jnp.where(at < 2 * width, near - width, far - 2 * width))
    moved = at + start
    total = jnp.zeros((n, g), F32)
    for k in range(3):
        total = total + jnp.where(slots_ref[k : k + 1, :] == moved, 1.0, 0.0)
    flipped_ref[...] = total.astype(BF16)
    counts_ref[...] = total.T.astype(BF16)
    for copy in copies:
        copy.wait()


def staged(slots, sources, grid_rows, nodes):
    shapes = [((grid_rows, nodes), BF16), ((nodes, grid_rows), BF16)]
    shapes += [(a.shape, a.dtype) for a in sources]
    return pl.pallas_call(
        stage_kernel,
        out_shape=[pltpu.VMEM(shape, dtype) for shape, dtype in shapes],
        in_specs=[VMEM] + [pl.BlockSpec(memory_space=pl.ANY)] * len(sources),
        out_specs=[VMEM] * len(shapes),
        scratch_shapes=[pltpu.SemaphoreType.DMA((len(sources),))],
        compiler_params=pltpu.CompilerParams(vmem_limit_bytes=grant),
    )(slots, *sources)


def forward_kernel(counts_ref, own_ref, rec_ref, fwd_ref, w_ref, wo_ref, turned_ref, gate_ref, pred_ref):
    extended = jnp.concatenate([own_ref[...], rec_ref[...], fwd_ref[...]], axis=0)
    area = dot(counts_ref[...], extended).astype(BF16)
    turned_ref[...] = area.T
    hidden = []
    for n in range(0, w_ref.shape[1], 2 * chunk):
        cols = slice(n, n + 2 * chunk)
        pre = dot(area, w_ref[:, cols])
        sig = 0.5 * jnp.tanh(0.5 * pre) + 0.5
        value = pre * sig
        gate_ref[:, cols] = (sig * (1.0 + (pre - value))).astype(BF16)
        hidden.append(value.astype(BF16))
    pred_ref[...] = dot(wo_ref[...], jnp.concatenate(hidden, axis=1), 1, 1).astype(BF16)


def smooth_sign(value):
    return value * lax.rsqrt(value * value + smooth_sq)


def half_slopes(start, half, wo_ref, gates, dps, slopes, turned, out):
    cols = pl.ds(pl.multiple_of(start, half), half)
    wo = wo_ref[:, cols]
    part = None
    for dp, gate, slope, area in zip(dps, gates, slopes, turned):
        value = (dot(dp[...], wo, 0, 0) * gate[:, cols].astype(F32)).astype(BF16)
        slope[...] = value
        more = dot(area[...], value)
        part = more if part is None else part + more
    out[...] = part.astype(out.dtype).reshape(out.shape)


def give_kernel(total, len_ref, *refs):
    preds, (target_ref, wo_ref, t0, t1, gate0, gate1, dp0, dp1, s0, s1, out) = refs[:8], refs[8:]
    channels, _ = target_ref.shape
    scale = (1.0 - fair_eps) / (total * (total - 1))
    for r in range(0, channels, 16):
        rows = slice(r, min(r + 16, channels))
        own = [preds[0][rows].astype(F32), preds[1][rows].astype(F32)]
        truth = target_ref[rows].astype(F32)
        mutual = smooth_sign(own[0] - own[1])
        pairs = [mutual, -mutual]
        for ref in preds[2:]:
            other = ref[rows].astype(F32)
            pairs = [p + smooth_sign(v - other) for p, v in zip(pairs, own)]
        at = lax.broadcasted_iota(jnp.int32, truth.shape, 1)
        for ref, v, p in zip((dp0, dp1), own, pairs):
            value = smooth_sign(v - truth) * (1.0 / total) - scale * p
            ref[rows] = jnp.where(at < len_ref[0], value, 0.0).astype(BF16)
    half = out.shape[-1]
    start = (1 - lax.axis_index("c")) * half
    half_slopes(start, half, wo_ref, (gate0, gate1), (dp0, dp1), (s0, s1), (t0, t1), out)


def keep_kernel(wo_ref, t0, t1, gate0, gate1, dp0, dp1, s0, s1, out):
    half = out.shape[-1]
    start = lax.axis_index("c") * half
    half_slopes(start, half, wo_ref, (gate0, gate1), (dp0, dp1), (s0, s1), (t0, t1), out)


def cores_kernel(keep_ref, got_ref, own_ref, *outs):
    wide = own_ref.shape[-1]
    for out, (a, b) in zip((own_ref,) + outs, ((0, 0), (0, 1), (1, 0), (1, 1))):
        xh = lax.rem(lax.axis_index("xh") + a, 2)
        xl = lax.rem(lax.axis_index("xl") + b, 2)
        cols = pl.ds(pl.multiple_of(xl * wide, wide), wide)
        out[...] = (
            keep_ref[:, xh, :, cols].astype(F32) + got_ref[:, xh, :, cols].astype(F32)
        ).astype(out.dtype)


def cut_kernel(first_ref, second_ref, third_ref, fourth_ref, own_ref, *outs):
    size = own_ref.shape[0]
    n_y = len(outs) + 1
    for s, out in enumerate((own_ref,) + outs):
        to = lax.rem(lax.axis_index("y") + s, n_y)
        at = pl.ds(to * size, size)
        total = first_ref[at]
        for ref in (second_ref, third_ref, fourth_ref):
            total = total + ref[at].astype(F32)
        out[...] = total.astype(out.dtype)


def total_kernel(first_ref, *refs):
    total = first_ref[...].astype(F32)
    for ref in refs[:-1]:
        total = total + ref[...].astype(F32)
    refs[-1][...] = total.astype(refs[-1].dtype)


def sum_kernel(parts_ref, out_ref):
    total = parts_ref[0].astype(F32)
    for k in range(1, parts_ref.shape[0]):
        total = total + parts_ref[k].astype(F32)
    out_ref[...] = total.astype(out_ref.dtype)


def place_kernel(mine_ref, x_ref, c_ref, both_ref, out_ref):
    wide = mine_ref.shape[1]
    c, xl = lax.axis_index("c"), lax.axis_index("xl")
    for k, ref in enumerate((mine_ref, x_ref, c_ref, both_ref)):
        at = lax.rem(c + k // 2, 2) * 2 + lax.rem(xl + k, 2)
        cols = pl.ds(pl.multiple_of(at * wide, wide), wide)
        out_ref[:, cols] = ref[...].astype(F32)


def join_kernel(rec0_ref, rec1_ref, far0_ref, far1_ref, out_ref):
    out_ref[0] = (rec0_ref[...] + far0_ref[...].astype(F32)).astype(BF16)
    out_ref[1] = (rec1_ref[...] + far1_ref[...].astype(F32)).astype(BF16)


def nodes_kernel(own0_ref, own1_ref, far_ref, out_ref):
    out_ref[0] = (own0_ref[...] + far_ref[0].astype(F32)).astype(BF16)
    out_ref[1] = (own1_ref[...] + far_ref[1].astype(F32)).astype(BF16)


def backward_kernel(flipped_ref, w_ref, give_ref, keep_ref, own_ref, rec_ref, fwd_ref):
    half = give_ref.shape[1]
    width = own_ref.shape[0]
    c = lax.axis_index("c")
    give = pl.ds(pl.multiple_of((1 - c) * half, half), half)
    keep = pl.ds(pl.multiple_of(c * half, half), half)
    for n in range(0, w_ref.shape[0], 2 * chunk):
        rows = slice(n, n + 2 * chunk)
        darea = dot(give_ref[...], w_ref[rows, give], 1, 1) + dot(keep_ref[...], w_ref[rows, keep], 1, 1)
        dext = dot(flipped_ref[...], darea.astype(BF16))
        own_ref[:, rows] = dext[:width]
        rec_ref[:, rows] = dext[width : 2 * width]
        fwd_ref[:, rows] = dext[2 * width :].astype(BF16)


def step(mesh_latent, w_hidden, w_out, target, slots, lengths):
    members, width, wide = mesh_latent.shape
    channels, grid_rows = target.shape
    total = members * lax.axis_size(MEMBER)
    half = wide // 2
    n_y, n_z, n_x = (lax.axis_size(a) for a in SPACE)

    own = [mesh_latent[m] for m in range(members)]
    rec = []
    for v in own:
        rec.append(shifted(v, "xh", 1))
    fwd = [relayed(v, 1) for v in rec]
    counts, flipped, w_hidden, w_out, target = staged(
        slots, (w_hidden, w_out, target), grid_rows, 3 * width
    )
    area, gate, pred = [], [], []
    for m in range(members):
        a, p, q = call(
            forward_kernel,
            [((wide, grid_rows), BF16), ((grid_rows, wide), BF16), ((channels, grid_rows), BF16)],
            counts, own[m], rec[m], fwd[m], w_hidden, w_out,
        )
        area.append(a)
        gate.append(p)
        pred.append(q)
    near, mate, last = [], [], []
    for m, q in enumerate(pred):
        near.append(shifted(q, "xl", 1))
        mate.append(shifted(q, "c", 1))
        last.append(shifted(near[m], "c", 1))
    others = near + mate + last

    slope = ((grid_rows, half), BF16)
    out_rows = wide // (n_y * n_z * n_x)
    part = ((n_y * n_z, n_x, out_rows, half), BF16)
    dp = ((channels, grid_rows), BF16)
    dp0, dp1, g0, g1, give = call(
        functools.partial(give_kernel, total), [dp, dp, slope, slope, part],
        lengths, *pred, *others, target, w_out, *area, *gate, scalars=1,
    )
    got = shifted(give, "c", 1)
    k0, k1, keep = call(keep_kernel, [slope, slope, part], w_out, *area, *gate, dp0, dp1)
    part = ((n_y * n_z, out_rows, half // 2), BF16)
    mine, *give = call(cores_kernel, [(part[0], F32)] + [part] * 3, keep, got)
    got = []
    give = (give[1], give[0], give[2])
    for axes, g in zip((("xh",), ("xl",), ("xl", "xh")), give):
        got.append(permute(g, axes, lambda *at: tuple(1 - i for i in at)))
    part = ((n_z, out_rows, half // 2), BF16)
    mine, *give = call(cut_kernel, [(part[0], F32)] + [part] * (n_y - 1), mine, *got)
    got = []
    for s in (2, 1, 3):
        got.append(shifted(give[s - 1], "y", s))
    (rows,) = call(total_kernel, [part], mine, *got)

    node = ((width, wide), F32)
    back = []
    for g, k in ((g0, k0), (g1, k1)):
        back.append(
            call(backward_kernel, [node, node, ((width, wide), BF16)], flipped, w_hidden, g, k)
        )
    far = []
    for b in back:
        far.append(relayed(b[2], -1))
    (far,) = call(join_kernel, [((members, width, wide), BF16)], *[b[1] for b in back], *far)
    far = shifted(far, "xh", 1)
    rows = lax.all_to_all(rows, "z", 0, 0)
    (mine,) = call(sum_kernel, [((out_rows, half // 2), BF16)], rows)
    quarters = []
    for axes in (("xl",), ("c",), MEMBER):
        quarters.append(permute(mine, axes, lambda *at: tuple(1 - i for i in at)))
    (grad_hidden,) = call(
        place_kernel, [((out_rows, wide), F32)], mine, *quarters, final=True
    )
    (grad_mesh,) = call(
        nodes_kernel, [((members, width, wide), BF16)], *[b[0] for b in back], far, final=True
    )
    return (grad_hidden, grad_mesh)


def solution(mesh):
    finer = Mesh(mesh.devices.reshape(2, 2, 4, 8, 2), NAMES)
    in_specs = (P(MEMBER, SPACE, None), P(), P(), P(None, SPACE), P(None, SPACE), P(SPACE))
    out_specs = (P(SPACE, None), P(MEMBER, SPACE, None))
    return jax.shard_map(step, mesh=finer, in_specs=in_specs, out_specs=out_specs, check_vma=False)
```

```python
import functools
import itertools

import jax
import jax.numpy as jnp
from jax import lax
from jax.experimental import pallas as pl
from jax.experimental.pallas import tpu as pltpu
from jax.sharding import Mesh
from jax.sharding import PartitionSpec as P

NAMES = ("xl", "c", "y", "z", "xh")
MEMBER = ("xl", "c")
SPACE = ("y", "z", "xh")
BF16 = jnp.bfloat16
F32 = jnp.float32
VMEM = pl.BlockSpec(memory_space=pltpu.VMEM)
SMEM = pl.BlockSpec(memory_space=pltpu.SMEM)
grant = 16 << 20

fair_eps = 0.05
smooth_sq = 0.01
chunk = 256


def permute(value, axes, moved):
    sizes = [lax.axis_size(a) for a in axes]
    pairs = []
    for at in itertools.product(*[range(s) for s in sizes]):
        source = target = 0
        for size, a, b in zip(sizes, at, moved(*at)):
            source, target = source * size + a, target * size + b % size
        pairs.append((source, target))
    return lax.ppermute(value, axes if len(axes) > 1 else axes[0], pairs)


def shifted(value, axis, steps):
    return permute(value, (axis,), lambda i: (i + steps,))


def relayed(value, sign):
    n_y, n_z = lax.axis_size("y"), lax.axis_size("z")

    def moved(y, z, xh):
        k = (y * n_z + z + (sign if xh == 0 else -sign)) % (n_y * n_z)
        return (k // n_z, k % n_z, xh)

    return permute(value, SPACE, moved)


def call(kernel, out_shape, *args, scalars=0, final=False):
    on_chip = [pltpu.with_memory_space_constraint(a, pltpu.VMEM) for a in args[scalars:]]
    return pl.pallas_call(
        kernel,
        out_shape=[
            jax.ShapeDtypeStruct(*s) if final else pltpu.VMEM(*s) for s in out_shape
        ],
        in_specs=[SMEM] * scalars + [VMEM] * len(on_chip),
        out_specs=[VMEM] * len(out_shape),
        compiler_params=pltpu.CompilerParams(vmem_limit_bytes=grant),
    )(*args[:scalars], *on_chip)


def dot(a, b, ca=1, cb=0):
    return lax.dot_general(a, b, (((ca,), (cb,)), ((), ())), preferred_element_type=F32)


def stage_kernel(slots_ref, *refs):
    sources, (counts_ref, flipped_ref, *targets, sems) = refs[:3], refs[3:]
    copies = [
        pltpu.make_async_copy(a, b, sems.at[k]) for k, (a, b) in enumerate(zip(sources, targets))
    ]
    for copy in copies:
        copy.start()
    n, g = flipped_ref.shape
    xh = lax.axis_index("xh")
    at = lax.broadcasted_iota(jnp.int32, (n, g), 0)
    width = n // 3
    far = jnp.where(xh == 0, 0, 2 * width)
    near = jnp.where(xh == 0, 2 * width, 0)
    start = jnp.where(at < width, width, jnp.where(at < 2 * width, near - width, far - 2 * width))
    moved = at + start
    total = jnp.zeros((n, g), F32)
    for k in range(3):
        total = total + jnp.where(slots_ref[k : k + 1, :] == moved, 1.0, 0.0)
    flipped_ref[...] = total.astype(BF16)
    counts_ref[...] = total.T.astype(BF16)
    for copy in copies:
        copy.wait()


def staged(slots, sources, grid_rows, nodes):
    shapes = [((grid_rows, nodes), BF16), ((nodes, grid_rows), BF16)]
    shapes += [(a.shape, a.dtype) for a in sources]
    return pl.pallas_call(
        stage_kernel,
        out_shape=[pltpu.VMEM(shape, dtype) for shape, dtype in shapes],
        in_specs=[VMEM] + [pl.BlockSpec(memory_space=pl.ANY)] * len(sources),
        out_specs=[VMEM] * len(shapes),
        scratch_shapes=[pltpu.SemaphoreType.DMA((len(sources),))],
        compiler_params=pltpu.CompilerParams(vmem_limit_bytes=grant),
    )(slots, *sources)


def forward_kernel(counts_ref, own_ref, rec_ref, fwd_ref, w_ref, wo_ref, turned_ref, gate_ref, pred_ref):
    extended = jnp.concatenate([own_ref[...], rec_ref[...], fwd_ref[...]], axis=0)
    area = dot(counts_ref[...], extended).astype(BF16)
    turned_ref[...] = area.T
    hidden = []
    for n in range(0, w_ref.shape[1], 2 * chunk):
        cols = slice(n, n + 2 * chunk)
        pre = dot(area, w_ref[:, cols])
        sig = 0.5 * jnp.tanh(0.5 * pre) + 0.5
        value = pre * sig
        gate_ref[:, cols] = (sig * (1.0 + (pre - value))).astype(BF16)
        hidden.append(value.astype(BF16))
    pred_ref[...] = dot(wo_ref[...], jnp.concatenate(hidden, axis=1), 1, 1).astype(BF16)


def smooth_sign(value):
    return value * lax.rsqrt(value * value + smooth_sq)


def half_slopes(start, half, wo_ref, gates, dps, slopes, turned, out):
    cols = pl.ds(pl.multiple_of(start, half), half)
    wo = wo_ref[:, cols]
    part = None
    for dp, gate, slope, area in zip(dps, gates, slopes, turned):
        value = (dot(dp[...], wo, 0, 0) * gate[:, cols].astype(F32)).astype(BF16)
        slope[...] = value
        more = dot(area[...], value)
        part = more if part is None else part + more
    out[...] = part.astype(out.dtype).reshape(out.shape)


def early_kernel(own0_ref, own1_ref, *refs):
    others, outs = refs[:-2], refs[-2:]
    for r in range(0, own0_ref.shape[0], 16):
        rows = slice(r, min(r + 16, own0_ref.shape[0]))
        own = [own0_ref[rows].astype(F32), own1_ref[rows].astype(F32)]
        mutual = smooth_sign(own[0] - own[1])
        pairs = [mutual, -mutual]
        for ref in others:
            other = ref[rows].astype(F32)
            pairs = [p + smooth_sign(v - other) for p, v in zip(pairs, own)]
        for ref, p in zip(outs, pairs):
            ref[rows] = p


def give_kernel(total, len_ref, *refs):
    sums, refs = refs[:2], refs[2:]
    preds, (target_ref, wo_ref, t0, t1, gate0, gate1, dp0, dp1, s0, s1, out) = refs[:5], refs[5:]
    channels, _ = target_ref.shape
    scale = (1.0 - fair_eps) / (total * (total - 1))
    for r in range(0, channels, 16):
        rows = slice(r, min(r + 16, channels))
        own = [preds[0][rows].astype(F32), preds[1][rows].astype(F32)]
        truth = target_ref[rows].astype(F32)
        pairs = [ref[rows] for ref in sums]
        for ref in preds[2:]:
            other = ref[rows].astype(F32)
            pairs = [p + smooth_sign(v - other) for p, v in zip(pairs, own)]
        at = lax.broadcasted_iota(jnp.int32, truth.shape, 1)
        for ref, v, p in zip((dp0, dp1), own, pairs):
            value = smooth_sign(v - truth) * (1.0 / total) - scale * p
            ref[rows] = jnp.where(at < len_ref[0], value, 0.0).astype(BF16)
    half = out.shape[-1]
    start = (1 - lax.axis_index("c")) * half
    half_slopes(start, half, wo_ref, (gate0, gate1), (dp0, dp1), (s0, s1), (t0, t1), out)


def keep_kernel(wo_ref, t0, t1, gate0, gate1, dp0, dp1, s0, s1, out):
    half = out.shape[-1]
    start = lax.axis_index("c") * half
    half_slopes(start, half, wo_ref, (gate0, gate1), (dp0, dp1), (s0, s1), (t0, t1), out)


def cores_kernel(keep_ref, got_ref, own_ref, *outs):
    wide = own_ref.shape[-1]
    for out, (a, b) in zip((own_ref,) + outs, ((0, 0), (0, 1), (1, 0), (1, 1))):
        xh = lax.rem(lax.axis_index("xh") + a, 2)
        xl = lax.rem(lax.axis_index("xl") + b, 2)
        cols = pl.ds(pl.multiple_of(xl * wide, wide), wide)
        out[...] = (
            keep_ref[:, xh, :, cols].astype(F32) + got_ref[:, xh, :, cols].astype(F32)
        ).astype(out.dtype)


def cut_kernel(first_ref, second_ref, third_ref, fourth_ref, own_ref, *outs):
    size = own_ref.shape[0]
    n_y = len(outs) + 1
    for s, out in enumerate((own_ref,) + outs):
        to = lax.rem(lax.axis_index("y") + s, n_y)
        at = pl.ds(to * size, size)
        total = first_ref[at]
        for ref in (second_ref, third_ref, fourth_ref):
            total = total + ref[at].astype(F32)
        out[...] = total.astype(out.dtype)


def total_kernel(first_ref, *refs):
    total = first_ref[...].astype(F32)
    for ref in refs[:-1]:
        total = total + ref[...].astype(F32)
    refs[-1][...] = total.astype(refs[-1].dtype)


def sum_kernel(parts_ref, out_ref):
    total = parts_ref[0].astype(F32)
    for k in range(1, parts_ref.shape[0]):
        total = total + parts_ref[k].astype(F32)
    out_ref[...] = total.astype(out_ref.dtype)


def place_kernel(mine_ref, x_ref, c_ref, both_ref, out_ref):
    wide = mine_ref.shape[1]
    c, xl = lax.axis_index("c"), lax.axis_index("xl")
    for k, ref in enumerate((mine_ref, x_ref, c_ref, both_ref)):
        at = lax.rem(c + k // 2, 2) * 2 + lax.rem(xl + k, 2)
        cols = pl.ds(pl.multiple_of(at * wide, wide), wide)
        out_ref[:, cols] = ref[...].astype(F32)


def join_kernel(rec0_ref, rec1_ref, far0_ref, far1_ref, out_ref):
    out_ref[0] = (rec0_ref[...] + far0_ref[...].astype(F32)).astype(BF16)
    out_ref[1] = (rec1_ref[...] + far1_ref[...].astype(F32)).astype(BF16)


def nodes_kernel(own0_ref, own1_ref, far_ref, out_ref):
    out_ref[0] = (own0_ref[...] + far_ref[0].astype(F32)).astype(BF16)
    out_ref[1] = (own1_ref[...] + far_ref[1].astype(F32)).astype(BF16)


def backward_kernel(flipped_ref, w_ref, give_ref, keep_ref, own_ref, rec_ref, fwd_ref):
    half = give_ref.shape[1]
    width = own_ref.shape[0]
    c = lax.axis_index("c")
    give = pl.ds(pl.multiple_of((1 - c) * half, half), half)
    keep = pl.ds(pl.multiple_of(c * half, half), half)
    for n in range(0, w_ref.shape[0], 2 * chunk):
        rows = slice(n, n + 2 * chunk)
        darea = dot(give_ref[...], w_ref[rows, give], 1, 1) + dot(keep_ref[...], w_ref[rows, keep], 1, 1)
        dext = dot(flipped_ref[...], darea.astype(BF16))
        own_ref[:, rows] = dext[:width]
        rec_ref[:, rows] = dext[width : 2 * width]
        fwd_ref[:, rows] = dext[2 * width :].astype(BF16)


def step(mesh_latent, w_hidden, w_out, target, slots, lengths):
    members, width, wide = mesh_latent.shape
    channels, grid_rows = target.shape
    total = members * lax.axis_size(MEMBER)
    half = wide // 2
    n_y, n_z, n_x = (lax.axis_size(a) for a in SPACE)

    own = [mesh_latent[m] for m in range(members)]
    rec = []
    for v in own:
        rec.append(shifted(v, "xh", 1))
    fwd = [relayed(v, 1) for v in rec]
    counts, flipped, w_hidden, w_out, target = staged(
        slots, (w_hidden, w_out, target), grid_rows, 3 * width
    )
    area, gate, pred = [], [], []
    for m in range(members):
        a, p, q = call(
            forward_kernel,
            [((wide, grid_rows), BF16), ((grid_rows, wide), BF16), ((channels, grid_rows), BF16)],
            counts, own[m], rec[m], fwd[m], w_hidden, w_out,
        )
        area.append(a)
        gate.append(p)
        pred.append(q)
    near, mate, last = [], [], []
    for m, q in enumerate(pred):
        near.append(shifted(q, "xl", 1))
        mate.append(shifted(q, "c", 1))
        last.append(shifted(near[m], "c", 1))
    sums = call(early_kernel, [((channels, grid_rows), F32)] * 2, *pred, near[0], *mate)
    others = [near[1]] + last

    slope = ((grid_rows, half), BF16)
    out_rows = wide // (n_y * n_z * n_x)
    part = ((n_y * n_z, n_x, out_rows, half), BF16)
    dp = ((channels, grid_rows), BF16)
    dp0, dp1, g0, g1, give = call(
        functools.partial(give_kernel, total), [dp, dp, slope, slope, part],
        lengths, *sums, *pred, *others, target, w_out, *area, *gate, scalars=1,
    )
    got = shifted(give, "c", 1)
    k0, k1, keep = call(keep_kernel, [slope, slope, part], w_out, *area, *gate, dp0, dp1)
    part = ((n_y * n_z, out_rows, half // 2), BF16)
    mine, *give = call(cores_kernel, [(part[0], F32)] + [part] * 3, keep, got)
    got = []
    give = (give[1], give[0], give[2])
    for axes, g in zip((("xh",), ("xl",), ("xl", "xh")), give):
        got.append(permute(g, axes, lambda *at: tuple(1 - i for i in at)))
    part = ((n_z, out_rows, half // 2), BF16)
    mine, *give = call(cut_kernel, [(part[0], F32)] + [part] * (n_y - 1), mine, *got)
    got = []
    for s in (2, 1, 3):
        got.append(shifted(give[s - 1], "y", s))
    (rows,) = call(total_kernel, [part], mine, *got)

    node = ((width, wide), F32)
    back = []
    for g, k in ((g0, k0), (g1, k1)):
        back.append(
            call(backward_kernel, [node, node, ((width, wide), BF16)], flipped, w_hidden, g, k)
        )
    far = []
    for b in back:
        far.append(relayed(b[2], -1))
    (far,) = call(join_kernel, [((members, width, wide), BF16)], *[b[1] for b in back], *far)
    far = shifted(far, "xh", 1)
    rows = lax.all_to_all(rows, "z", 0, 0)
    (mine,) = call(sum_kernel, [((out_rows, half // 2), BF16)], rows)
    quarters = []
    for axes in (("xl",), ("c",), MEMBER):
        quarters.append(permute(mine, axes, lambda *at: tuple(1 - i for i in at)))
    (grad_hidden,) = call(
        place_kernel, [((out_rows, wide), F32)], mine, *quarters, final=True
    )
    (grad_mesh,) = call(
        nodes_kernel, [((members, width, wide), BF16)], *[b[0] for b in back], far, final=True
    )
    return (grad_hidden, grad_mesh)


def solution(mesh):
    finer = Mesh(mesh.devices.reshape(2, 2, 4, 8, 2), NAMES)
    in_specs = (P(MEMBER, SPACE, None), P(), P(), P(None, SPACE), P(None, SPACE), P(SPACE))
    out_specs = (P(SPACE, None), P(MEMBER, SPACE, None))
    return jax.shard_map(step, mesh=finer, in_specs=in_specs, out_specs=out_specs, check_vma=False)
```
